32 devices in a mesh: dp: 2 (over x), ctx: 4 (over z), tensor: 4 (over y, core).
Axes of the slice: x: 2, y: 2, z: 4, core: 2. Of those that a mesh axis runs over, the one named last changes fastest.
Arguments:
- query_rows: bfloat16 [2, 1024, 5120], P('dp', 'ctx', 'tensor'), may hold values from -6 to 6
- key_rows: bfloat16 [2, 1024, 5120], P('dp', 'ctx', 'tensor'), may hold values from -6 to 6
- value_rows: bfloat16 [2, 1024, 5120], P('dp', 'ctx', 'tensor'), may hold values from -6 to 6
- decay_exp: int32 [40], P('tensor'), may hold values from 1 to 32768, as said below
- out_grad: bfloat16 [2, 1024, 5120], P('dp', 'ctx', 'tensor'), may hold values from -6 to 6
- gain_weight: bfloat16 [40, 128], P('tensor'), may hold values from 0.5 to 1.5
- master_gain: float32 [40, 128], P('tensor', ('dp', 'ctx')), may hold values from 0.5 to 1.5
- first_moment: float32 [40, 128], P('tensor', ('dp', 'ctx')), may hold values from -3 to 3
- second_moment: float32 [40, 128], P('tensor', ('dp', 'ctx')), may hold values from 0.25 to 4
Outputs:
- attn_out: bfloat16 [2, 1024, 5120], P('dp', 'ctx', 'tensor')
- query_grad: bfloat16 [2, 1024, 5120], P('dp', 'ctx', 'tensor')
- key_grad: bfloat16 [2, 1024, 5120], P('dp', 'ctx', 'tensor')
- value_grad: bfloat16 [2, 1024, 5120], P('dp', 'ctx', 'tensor')
- master_new: float32 [40, 128], P('tensor', ('dp', 'ctx'))
- moment_new: float32 [40, 128], P('tensor', ('dp', 'ctx'))
- second_new: float32 [40, 128], P('tensor', ('dp', 'ctx'))
The draws below stay inside these ranges and needn't reach their ends.
Inputs may be any that keep to these rules, and one draw needn't show every extreme that they name: `decay_exp`: each exponent is a power of two, 2^k with k in 0 to 3 or in 8 to 15.
All inputs are finite; a program needn't handle non-finite values.
Results may differ from the reference program's by a relative error of at most 0.0064.
Values sent between devices are 32-bit elements; how exact they have to be, the bound alone decides.
A program may use at most 64 MiB of HBM per device.

```python
import math
import jax
import jax.numpy as jnp
from jax import lax

BLOCK = 256
HEAD_DIM = 128
H = 40
SEQ = 1024
BATCH = 2
TOKENS = 2048


def draw_decay_exp(key, part):
    shuffled = jax.random.permutation(key, H)
    levels = shuffled % 16
    powers = jnp.where(levels < 8, levels // 2, levels)
    return jnp.left_shift(jnp.ones_like(powers), powers).astype(jnp.int32)


def block_scale(rng, dims, shards, low, top_value):
    level = 1.0
    for dim, shards_of in shards:
        steps = jax.random.uniform(jax.random.fold_in(jax.random.fold_in(rng, 6), dim), (shards_of,), jnp.float32, low / len(shards), top_value / len(shards))
        level = level * jnp.repeat(jnp.exp(steps), dims[dim] // shards_of).reshape((-1,) + (1,) * (len(dims) - 1 - dim))
    return level


def gaussian(key, dims, width, most, pieces=(), kind=jnp.bfloat16):
    drawn = width * jax.random.normal(key, dims, jnp.float32)
    if pieces:
        drawn = drawn * block_scale(key, dims, pieces, -0.22, 0.18)
    return jnp.clip(drawn, -most, most).astype(kind)


def setup_inputs(seed: int = 0) -> dict:
    arg_keys = jax.random.split(jax.random.key(seed), 10)
    return {
        "query_rows": gaussian(arg_keys[0], (BATCH, SEQ, H * HEAD_DIM), 1.0, 6.0, ((0, 2), (1, 4), (2, 4))),
        "key_rows": gaussian(arg_keys[1], (BATCH, SEQ, H * HEAD_DIM), 1.0, 6.0, ((0, 2), (1, 4), (2, 4))),
        "value_rows": gaussian(arg_keys[2], (BATCH, SEQ, H * HEAD_DIM), 1.0, 6.0, ((0, 2), (1, 4), (2, 4))),
        "decay_exp": draw_decay_exp(jax.random.fold_in(arg_keys[9], 71), 0),
        "out_grad": gaussian(arg_keys[4], (BATCH, SEQ, H * HEAD_DIM), 1.0, 6.0, ((0, 2), (1, 4), (2, 4))),
        "gain_weight": jnp.clip(0.5 + 1.0 * jax.random.uniform(arg_keys[5], (H, HEAD_DIM), jnp.float32) ** block_scale(arg_keys[5], (H, HEAD_DIM), ((0, 4),), -0.2, 0.2), 0.5, 1.5).astype(jnp.bfloat16),
        "master_gain": jnp.clip(0.5 + 1.0 * jax.random.uniform(arg_keys[6], (H, HEAD_DIM), jnp.float32) ** block_scale(arg_keys[6], (H, HEAD_DIM), ((0, 4), (1, 8)), -0.2, 0.2), 0.5, 1.5),
        "first_moment": gaussian(arg_keys[7], (H, HEAD_DIM), 0.5, 3.0, ((0, 4), (1, 8)), jnp.float32),
        "second_moment": jnp.clip(jnp.exp(math.log(4.0) - 2.7725887 * jax.random.uniform(arg_keys[8], (H, HEAD_DIM), jnp.float32) ** block_scale(arg_keys[8], (H, HEAD_DIM), ((0, 4), (1, 8)), -0.2, 0.2)), 0.25, 4.0),
    }


beta_one = 0.9
beta_two = 0.95
learn_rate = 0.02
adam_eps = 1e-08
bias_one = 0.9999734386011124
bias_two = 0.9940794707796667
norm_eps = 1e-05

def rounded(value):
    return lax.optimization_barrier(value.astype(jnp.bfloat16)).astype(jnp.float32)

def decay_tables(decay_rate):
    position = jnp.arange(BLOCK, dtype=jnp.float32)
    gap_len = position[:, None] - position[None, :]
    decay_mask = jnp.where(gap_len >= 0, jnp.exp(-decay_rate[:, None, None] * jnp.maximum(gap_len, 0.0)), 0.0)
    query_decay = jnp.exp(-decay_rate[:, None] * position[None, :])
    key_decay = jnp.exp(-decay_rate[:, None] * (BLOCK - position)[None, :])
    block_decay = jnp.exp(-decay_rate * BLOCK)
    return (decay_mask, query_decay, key_decay, block_decay)

def to_blocks(rows):
    return rows.reshape(BATCH, SEQ // BLOCK, BLOCK, H, HEAD_DIM).transpose(1, 0, 3, 2, 4)

def from_blocks(parts):
    return parts.transpose(1, 0, 3, 2, 4).reshape(BATCH, SEQ, H * HEAD_DIM)

def reference(query_rows, key_rows, value_rows, decay_exp, out_grad, gain_weight, master_gain, first_moment, second_moment):
    decay_rate = decay_exp.astype(jnp.float32) * (math.log(2.0) / (4.0 * SEQ))
    decay_mask, query_decay, key_decay, block_decay = decay_tables(decay_rate)
    mask_rows = decay_mask[None]
    query_dec = query_decay[None, :, :, None]
    key_dec = key_decay[None, :, :, None]
    step_dec = block_decay[None, :, None, None]
    query_blocks = to_blocks(query_rows)
    key_blocks = to_blocks(key_rows)
    value_blocks = to_blocks(value_rows)

    def forward_step(run_state, step_items):
        query_blk = step_items[0].astype(jnp.float32)
        key_blk = step_items[1].astype(jnp.float32)
        value_blk = step_items[2].astype(jnp.float32)
        scores = jnp.einsum('bhtd,bhsd->bhts', query_blk, key_blk)
        weights = rounded(scores * mask_rows)
        state_low = rounded(run_state)
        attn_blk = jnp.einsum('bhts,bhsd->bhtd', weights, value_blk)
        attn_blk = attn_blk + query_dec * jnp.einsum('bhtd,bhde->bhte', query_blk, state_low)
        key_scaled = rounded(key_dec * key_blk)
        run_state = step_dec * run_state + jnp.einsum('bhsd,bhse->bhde', key_scaled, value_blk)
        return (run_state, (attn_blk, state_low.astype(jnp.bfloat16)))
    zero_state = jnp.zeros((BATCH, H, HEAD_DIM, HEAD_DIM), jnp.float32)
    _, (attn_blocks, state_blocks) = lax.scan(forward_step, zero_state, (query_blocks, key_blocks, value_blocks))
    attn_all = from_blocks(attn_blocks)
    gain_flat = gain_weight.reshape(-1).astype(jnp.float32)
    inv_rms = lax.rsqrt(lax.optimization_barrier(jnp.mean(attn_all * attn_all, axis=-1, keepdims=True)) + norm_eps)
    attn_out = (gain_flat * attn_all * inv_rms).astype(jnp.bfloat16)
    grad_full = out_grad.astype(jnp.float32)
    scaled_grad = grad_full * gain_flat
    mean_dot = lax.optimization_barrier(jnp.mean(scaled_grad * attn_all, axis=-1, keepdims=True))
    grad_low = (inv_rms * (scaled_grad - attn_all * inv_rms * inv_rms * mean_dot)).astype(jnp.bfloat16)
    gain_grad = lax.optimization_barrier(jnp.sum(grad_full * attn_all * inv_rms, axis=(0, 1))).reshape(H, HEAD_DIM) / math.sqrt(TOKENS)
    grad_blocks = to_blocks(grad_low)

    def backward_step(back_carry, step_items):
        query_blk = step_items[0].astype(jnp.float32)
        key_blk = step_items[1].astype(jnp.float32)
        value_blk = step_items[2].astype(jnp.float32)
        grad_blk = step_items[3].astype(jnp.float32)
        state_low = step_items[4].astype(jnp.float32)
        scores = jnp.einsum('bhtd,bhsd->bhts', query_blk, key_blk)
        weights = rounded(scores * mask_rows)
        back_low = rounded(back_carry)
        dweights = rounded(jnp.einsum('bhte,bhse->bhts', grad_blk, value_blk) * mask_rows)
        query_part = jnp.einsum('bhts,bhsd->bhtd', dweights, key_blk) + query_dec * jnp.einsum('bhte,bhde->bhtd', grad_blk, state_low)
        key_part = jnp.einsum('bhts,bhtd->bhsd', dweights, query_blk) + key_dec * jnp.einsum('bhse,bhde->bhsd', value_blk, back_low)
        value_part = jnp.einsum('bhts,bhte->bhse', weights, grad_blk) + key_dec * jnp.einsum('bhsd,bhde->bhse', key_blk, back_low)
        query_scaled = rounded(query_dec * query_blk)
        back_carry = step_dec * back_carry + jnp.einsum('bhtd,bhte->bhde', query_scaled, grad_blk)
        return (back_carry, (query_part.astype(jnp.bfloat16), key_part.astype(jnp.bfloat16), value_part.astype(jnp.bfloat16)))
    _, (query_parts, key_parts, value_parts) = lax.scan(backward_step, zero_state, (query_blocks, key_blocks, value_blocks, grad_blocks, state_blocks), reverse=True)
    moment_new = beta_one * first_moment + (1.0 - beta_one) * gain_grad
    second_new = beta_two * second_moment + (1.0 - beta_two) * gain_grad * gain_grad
    master_new = master_gain - learn_rate * (moment_new / bias_one) / (jnp.sqrt(second_new / bias_two) + adam_eps)
    return (attn_out, from_blocks(query_parts), from_blocks(key_parts), from_blocks(value_parts), master_new, moment_new, second_new)
```

```python
import functools
import math

import jax
import jax.numpy as jnp
from jax import lax
from jax.experimental import pallas as pl
from jax.experimental.pallas import tpu as pltpu
from jax.sharding import PartitionSpec as P

HEAD_DIM = 128
MESH = pl.DeviceIdType.MESH

beta_one = 0.9
beta_two = 0.95
learn_rate = 0.02
adam_eps = 1e-08
bias_one = 0.9999734386011124
bias_two = 0.9940794707796667
norm_eps = 1e-05

LOW = jnp.bfloat16
F32 = jnp.float32


def dot(a, b, dim_a, dim_b, precision=None):
    return lax.dot_general(
        a, b, (((dim_a,), (dim_b,)), ((), ())), preferred_element_type=F32, precision=precision
    )


def fused(
    dims,
    exp_ref,
    query_hbm,
    key_hbm,
    value_hbm,
    grad_hbm,
    gain_ref,
    master_ref,
    first_ref,
    second_ref,
    attn_hbm,
    qgrad_hbm,
    kgrad_hbm,
    vgrad_hbm,
    master_out,
    moment_out,
    second_out,
    query_v,
    key_v,
    value_v,
    grad_v,
    attn_v,
    mask_v,
    weight_v,
    low_v,
    local_v,
    fwd_in,
    fwd_out,
    bwd_in,
    bwd_out,
    gl_v,
    ao_v,
    qg_v,
    kg_v,
    vg_v,
    gain_v,
    gpart_v,
    square_acc,
    dot_acc,
    norm_mine,
    norm_in,
    ctx_in,
    dp_mine,
    dp_in,
    in_sem,
    out_sem,
    fs_sem,
    fr_sem,
    bs_sem,
    br_sem,
    ts_sem,
    tr_sem,
    cs_sem,
    cr_sem,
    ds_sem,
    dr_sem,
):
    heads, length, n_dp, n_ctx, n_tensor = dims
    seq_len = length * n_ctx
    channels = heads * HEAD_DIM * n_tensor
    token_count = n_dp * seq_len
    at_dp, at_ctx, at_tensor = (lax.axis_index(name) for name in ("dp", "ctx", "tensor"))
    later = lax.rem(at_ctx + 1, n_ctx)
    earlier = lax.rem(at_ctx + n_ctx - 1, n_ctx)
    is_first, is_last = at_ctx == 0, at_ctx == n_ctx - 1

    def columns(h):
        return pl.ds(pl.multiple_of(h * HEAD_DIM, HEAD_DIM), HEAD_DIM)

    pairs = ((key_hbm, key_v), (value_hbm, value_v), (query_hbm, query_v), (grad_hbm, grad_v))

    def load(which, h):
        hbm, vmem = pairs[which]
        return pltpu.make_async_copy(hbm.at[:, columns(h)], vmem.at[h], in_sem.at[which, h])

    outs = ((ao_v, attn_hbm), (qg_v, qgrad_hbm), (kg_v, kgrad_hbm), (vg_v, vgrad_hbm))

    def save(which, h):
        vmem, hbm = outs[which]
        return pltpu.make_async_copy(vmem.at[h], hbm.at[:, columns(h)], out_sem.at[which, h])

    def loop(low, high, step):
        lax.fori_loop(low, high, lambda h, c: (step(h), c)[1], 0)

    def start_kv(h):
        load(0, h).start()
        load(1, h).start()

    def start_qg(h):
        load(2, h).start()
        load(3, h).start()

    loop(0, heads, start_kv)
    loop(0, heads, start_qg)

    barrier = pltpu.get_barrier_semaphore()
    groups = (("dp", at_dp, n_dp), ("ctx", at_ctx, n_ctx), ("tensor", at_tensor, n_tensor))
    for name, mine, count in groups:
        for d in range(1, count):
            pl.semaphore_signal(
                barrier, inc=1, device_id={name: lax.rem(mine + d, count)}, device_id_type=MESH
            )
    pl.semaphore_wait(barrier, n_dp + n_ctx + n_tensor - 3)

    def share(name, mine, count, source, slots, send_sem, recv_sem):
        return [
            pltpu.make_async_remote_copy(
                src_ref=source,
                dst_ref=slots.at[d - 1],
                send_sem=send_sem.at[d - 1],
                recv_sem=recv_sem.at[d - 1],
                device_id={name: lax.rem(mine + d, count)},
                device_id_type=MESH,
            )
            for d in range(1, count)
        ]

    def forward_copy(h):
        return pltpu.make_async_remote_copy(
            src_ref=fwd_out.at[h],
            dst_ref=fwd_in.at[h],
            send_sem=fs_sem.at[h],
            recv_sem=fr_sem.at[h],
            device_id={"ctx": later},
            device_id_type=MESH,
        )

    def backward_copy(h):
        return pltpu.make_async_remote_copy(
            src_ref=bwd_out.at[h],
            dst_ref=bwd_in.at[h],
            send_sem=bs_sem.at[h],
            recv_sem=br_sem.at[h],
            device_id={"ctx": earlier},
            device_id_type=MESH,
        )

    gain_v[...] = gain_ref[...].astype(F32)
    row = lax.broadcasted_iota(jnp.int32, (length, HEAD_DIM), 0).astype(F32)

    def rate_of(h):
        return exp_ref[h].astype(F32) * (math.log(2.0) / (4.0 * seq_len))

    def key_decay(h):
        return jnp.exp(-rate_of(h) * (length - row))

    def query_decay(h):
        return jnp.exp(-rate_of(h) * row)

    def block_decay(h):
        return jnp.exp(jnp.full((HEAD_DIM, HEAD_DIM), -rate_of(h) * length, F32))

    def summarize(h):
        load(0, h).wait()
        load(1, h).wait()
        scaled = (key_decay(h) * key_v[h].astype(F32)).astype(LOW)
        summary = dot(scaled, value_v[h], 0, 0)

        @pl.when(is_first)
        def _():
            fwd_out[h] = summary
            forward_copy(h).start()

        @pl.when(jnp.logical_not(is_first))
        def _():
            local_v[h] = summary

    loop(0, heads, summarize)
    square_acc[...] = jnp.zeros_like(square_acc)
    dot_acc[...] = jnp.zeros_like(dot_acc)

    def attend(h):
        load(2, h).wait()
        load(3, h).wait()
        gap = (
            lax.broadcasted_iota(jnp.int32, (length, length), 0)
            - lax.broadcasted_iota(jnp.int32, (length, length), 1)
        ).astype(F32)
        mask = jnp.where(gap >= 0, jnp.exp(-rate_of(h) * jnp.maximum(gap, 0.0)), 0.0)
        mask_v[h] = mask
        query = query_v[h]
        weights = (dot(query, key_v[h], 1, 1) * mask).astype(LOW)
        weight_v[h] = weights
        attn_v[h] = dot(weights, value_v[h], 1, 0)

        @pl.when(is_first)
        def _():
            low_v[h] = jnp.zeros((HEAD_DIM, HEAD_DIM), LOW)

        @pl.when(jnp.logical_not(is_first))
        def _():
            forward_copy(h).wait_recv()

            @pl.when(jnp.logical_not(is_last))
            def _():
                fwd_out[h] = block_decay(h) * fwd_in[h] + local_v[h]
                forward_copy(h).start()

            low_v[h] = fwd_in[h].astype(LOW)

        attn = attn_v[h] + query_decay(h) * dot(query_v[h], low_v[h], 1, 0)
        attn_v[h] = attn
        square_acc[...] += attn * attn
        dot_acc[...] += grad_v[h].astype(F32) * gain_v[pl.ds(h, 1), :] * attn

    loop(0, heads, attend)

    exact = lax.Precision.HIGHEST
    ones = jnp.ones((8, HEAD_DIM), F32)
    upper = lax.broadcasted_iota(jnp.int32, (8, length), 0) < 4
    norm_mine[...] = jnp.where(
        upper, dot(ones, square_acc[...], 1, 1, exact), dot(ones, dot_acc[...], 1, 1, exact)
    )
    norm_copies = share("tensor", at_tensor, n_tensor, norm_mine, norm_in, ts_sem, tr_sem)
    for copy in norm_copies:
        copy.start()
    total = norm_mine[...]
    for d, copy in enumerate(norm_copies):
        copy.wait_recv()
        total = total + norm_in[d]
    pick = lax.broadcasted_iota(jnp.int32, (8, HEAD_DIM), 0)
    square_sum = dot(total, (pick == 0).astype(F32), 0, 0, exact)
    dot_sum = dot(total, (pick == 4).astype(F32), 0, 0, exact)
    inv_rms = lax.rsqrt(square_sum / channels + norm_eps)
    mean_dot = dot_sum / channels
    square_acc[...] = inv_rms
    dot_acc[...] = inv_rms * inv_rms * mean_dot

    def back_summary(h):
        attn = attn_v[h]
        inverse = square_acc[...]
        gain = gain_v[pl.ds(h, 1), :]
        grad = grad_v[h].astype(F32)
        grad_low = (inverse * (grad * gain - attn * dot_acc[...])).astype(LOW)
        gl_v[h] = grad_low
        scaled = (query_decay(h) * query_v[h].astype(F32)).astype(LOW)
        part = dot(scaled, grad_low, 0, 0)

        @pl.when(is_last)
        def _():
            bwd_out[h] = part
            backward_copy(h).start()

        @pl.when(jnp.logical_not(is_last))
        def _():
            local_v[h] = part

        normed = attn * inverse
        ao_v[h] = (gain * normed).astype(LOW)
        save(0, h).start()
        gpart_v[pl.ds(h, 1), :] = jnp.sum(grad * normed, axis=0, keepdims=True)

    loop(0, heads, back_summary)
    ctx_copies = share("ctx", at_ctx, n_ctx, gpart_v, ctx_in, cs_sem, cr_sem)
    for copy in ctx_copies:
        copy.start()

    def gradients(h):
        grad_low = gl_v[h]
        dweights = (dot(grad_low, value_v[h], 1, 1) * mask_v[h]).astype(LOW)
        query_part = dot(dweights, key_v[h], 1, 0)
        query_part += query_decay(h) * dot(grad_low, low_v[h], 1, 1)
        qg_v[h] = query_part.astype(LOW)
        save(1, h).start()
        key_part = dot(dweights, query_v[h], 0, 0)
        value_part = dot(weight_v[h], grad_low, 0, 0)

        @pl.when(is_last)
        def _():
            kg_v[h] = key_part.astype(LOW)
            vg_v[h] = value_part.astype(LOW)

        @pl.when(jnp.logical_not(is_last))
        def _():
            backward_copy(h).wait_recv()

            @pl.when(jnp.logical_not(is_first))
            def _():
                bwd_out[h] = block_decay(h) * bwd_in[h] + local_v[h]
                backward_copy(h).start()

            back_low = bwd_in[h].astype(LOW)
            decay = key_decay(h)
            kg_v[h] = (key_part + decay * dot(value_v[h], back_low, 1, 1)).astype(LOW)
            vg_v[h] = (value_part + decay * dot(key_v[h], back_low, 1, 0)).astype(LOW)

        save(2, h).start()
        save(3, h).start()

    third = heads // 3
    loop(0, third, gradients)
    gain_sum = gpart_v[...]
    for d, copy in enumerate(ctx_copies):
        copy.wait_recv()
        gain_sum = gain_sum + ctx_in[d]
    dp_mine[...] = gain_sum
    dp_copies = share("dp", at_dp, n_dp, dp_mine, dp_in, ds_sem, dr_sem)
    for copy in dp_copies:
        copy.start()
    loop(third, heads - 1, gradients)

    gain_sum = dp_mine[...]
    for d, copy in enumerate(dp_copies):
        copy.wait_recv()
        gain_sum = gain_sum + dp_in[d]
    width = master_ref.shape[1]
    place = (at_dp * n_ctx + at_ctx) * width
    chosen = lax.broadcasted_iota(jnp.int32, (HEAD_DIM, width), 0) == (
        lax.broadcasted_iota(jnp.int32, (HEAD_DIM, width), 1) + place
    )
    gain_grad = dot(gain_sum, chosen.astype(F32), 1, 0, exact) / math.sqrt(token_count)
    moment_new = beta_one * first_ref[...] + (1.0 - beta_one) * gain_grad
    second_new = beta_two * second_ref[...] + (1.0 - beta_two) * gain_grad * gain_grad
    moment_out[...] = moment_new
    second_out[...] = second_new
    master_out[...] = master_ref[...] - learn_rate * (moment_new / bias_one) / (
        jnp.sqrt(second_new / bias_two) + adam_eps
    )

    loop(heads - 1, heads, gradients)

    def finish(h):
        for which in range(4):
            save(which, h).wait()

        @pl.when(jnp.logical_not(is_last))
        def _():
            forward_copy(h).wait_send()

        @pl.when(jnp.logical_not(is_first))
        def _():
            backward_copy(h).wait_send()

    loop(0, heads, finish)
    for copy in norm_copies + ctx_copies + dp_copies:
        copy.wait_send()


def body(
    mesh_dims,
    query_rows,
    key_rows,
    value_rows,
    decay_exp,
    out_grad,
    gain_weight,
    master_gain,
    first_moment,
    second_moment,
):
    _, length, row_width = query_rows.shape
    heads = row_width // HEAD_DIM
    n_dp, n_ctx, n_tensor = mesh_dims
    rows = (length, row_width)
    tile = (heads, length, HEAD_DIM)
    state = (heads, HEAD_DIM, HEAD_DIM)
    gain_dims = (heads, HEAD_DIM)
    any_spec = pl.BlockSpec(memory_space=pl.ANY)
    vmem_spec = pl.BlockSpec(memory_space=pltpu.VMEM)
    dma = pltpu.SemaphoreType.DMA
    scratch = (
        [pltpu.VMEM(tile, LOW)] * 4
        + [
            pltpu.VMEM(tile, F32),
            pltpu.VMEM((heads, length, length), F32),
            pltpu.VMEM((heads, length, length), LOW),
            pltpu.VMEM(state, LOW),
        ]
        + [pltpu.VMEM(state, F32)] * 5
        + [pltpu.VMEM(tile, LOW)] * 5
        + [
            pltpu.VMEM(gain_dims, F32),
            pltpu.VMEM(gain_dims, F32),
            pltpu.VMEM((length, HEAD_DIM), F32),
            pltpu.VMEM((length, HEAD_DIM), F32),
            pltpu.VMEM((8, length), F32),
            pltpu.VMEM((n_tensor - 1, 8, length), F32),
            pltpu.VMEM((n_ctx - 1,) + gain_dims, F32),
            pltpu.VMEM(gain_dims, F32),
            pltpu.VMEM((n_dp - 1,) + gain_dims, F32),
            dma((4, heads)),
            dma((4, heads)),
            dma((heads,)),
            dma((heads,)),
            dma((heads,)),
            dma((heads,)),
            dma((n_tensor - 1,)),
            dma((n_tensor - 1,)),
            dma((n_ctx - 1,)),
            dma((n_ctx - 1,)),
            dma((n_dp - 1,)),
            dma((n_dp - 1,)),
        ]
    )
    results = pl.pallas_call(
        functools.partial(fused, (heads, length, n_dp, n_ctx, n_tensor)),
        out_shape=[jax.ShapeDtypeStruct(rows, LOW)] * 4
        + [jax.ShapeDtypeStruct(master_gain.shape, F32)] * 3,
        in_specs=[pl.BlockSpec(memory_space=pltpu.SMEM)] + [any_spec] * 4 + [vmem_spec] * 4,
        out_specs=[any_spec] * 4 + [vmem_spec] * 3,
        scratch_shapes=scratch,
        compiler_params=pltpu.CompilerParams(
            collective_id=0, has_side_effects=True, vmem_limit_bytes=48 * 1024 * 1024
        ),
        name="fused",
    )(
        decay_exp,
        query_rows.reshape(rows),
        key_rows.reshape(rows),
        value_rows.reshape(rows),
        out_grad.reshape(rows),
        gain_weight,
        master_gain,
        first_moment,
        second_moment,
    )
    full = tuple(part.reshape(query_rows.shape) for part in results[:4])
    return full + tuple(results[4:])


def solution(mesh):
    rows = P("dp", "ctx", "tensor")
    share = P("tensor", ("dp", "ctx"))
    mesh_dims = (mesh.shape["dp"], mesh.shape["ctx"], mesh.shape["tensor"])
    return jax.shard_map(
        functools.partial(body, mesh_dims),
        mesh=mesh,
        in_specs=(rows, rows, rows, P("tensor"), rows, P("tensor", None), share, share, share),
        out_specs=(rows, rows, rows, rows, share, share, share),
        check_vma=False,
    )
```

```python
import functools
import math

import jax
import jax.numpy as jnp
from jax import lax
from jax.experimental import pallas as pl
from jax.experimental.pallas import tpu as pltpu
from jax.sharding import PartitionSpec as P

HEAD_DIM = 128
MESH = pl.DeviceIdType.MESH

beta_one = 0.9
beta_two = 0.95
learn_rate = 0.02
adam_eps = 1e-08
bias_one = 0.9999734386011124
bias_two = 0.9940794707796667
norm_eps = 1e-05

LOW = jnp.bfloat16
F32 = jnp.float32


def dot(a, b, dim_a, dim_b, precision=None):
    return lax.dot_general(
        a, b, (((dim_a,), (dim_b,)), ((), ())), preferred_element_type=F32, precision=precision
    )


def fused(
    dims,
    exp_hbm,
    query_hbm,
    key_hbm,
    value_hbm,
    grad_hbm,
    gain_hbm,
    master_hbm,
    first_hbm,
    second_hbm,
    attn_out,
    qgrad_out,
    kgrad_out,
    vgrad_out,
    master_out,
    moment_out,
    second_out,
    exp_ref,
    query_v,
    key_v,
    value_v,
    grad_v,
    gain_ref,
    master_ref,
    first_ref,
    second_ref,
    attn_v,
    mask_v,
    weight_v,
    low_v,
    local_v,
    fwd_in,
    fwd_out,
    bwd_in,
    bwd_out,
    gl_v,
    gain_v,
    gpart_v,
    square_acc,
    dot_acc,
    norm_mine,
    norm_in,
    ctx_in,
    dp_mine,
    dp_in,
    in_sem,
    fs_sem,
    fr_sem,
    bs_sem,
    br_sem,
    ts_sem,
    tr_sem,
    cs_sem,
    cr_sem,
    ds_sem,
    dr_sem,
):
    heads, length, n_dp, n_ctx, n_tensor = dims
    seq_len = length * n_ctx
    channels = heads * HEAD_DIM * n_tensor
    token_count = n_dp * seq_len
    at_dp, at_ctx, at_tensor = (lax.axis_index(name) for name in ("dp", "ctx", "tensor"))
    later = lax.rem(at_ctx + 1, n_ctx)
    earlier = lax.rem(at_ctx + n_ctx - 1, n_ctx)
    is_first, is_last = at_ctx == 0, at_ctx == n_ctx - 1

    def columns(h):
        return pl.ds(pl.multiple_of(h * HEAD_DIM, HEAD_DIM), HEAD_DIM)

    pairs = (
        (exp_hbm, exp_ref),
        (key_hbm, key_v),
        (value_hbm, value_v),
        (query_hbm, query_v),
        (grad_hbm, grad_v),
        (gain_hbm, gain_ref),
        (master_hbm, master_ref),
        (first_hbm, first_ref),
        (second_hbm, second_ref),
    )
    loads = [
        pltpu.make_async_copy(hbm, local, in_sem.at[i]) for i, (hbm, local) in enumerate(pairs)
    ]
    for copy in loads:
        copy.start()

    def loop(low, high, step):
        lax.fori_loop(low, high, lambda h, c: (step(h), c)[1], 0)

    barrier = pltpu.get_barrier_semaphore()
    groups = (("dp", at_dp, n_dp), ("ctx", at_ctx, n_ctx), ("tensor", at_tensor, n_tensor))
    for name, mine, count in groups:
        for d in range(1, count):
            pl.semaphore_signal(
                barrier, inc=1, device_id={name: lax.rem(mine + d, count)}, device_id_type=MESH
            )
    pl.semaphore_wait(barrier, n_dp + n_ctx + n_tensor - 3)

    def share(name, mine, count, source, slots, send_sem, recv_sem):
        return [
            pltpu.make_async_remote_copy(
                src_ref=source,
                dst_ref=slots.at[d - 1],
                send_sem=send_sem.at[d - 1],
                recv_sem=recv_sem.at[d - 1],
                device_id={name: lax.rem(mine + d, count)},
                device_id_type=MESH,
            )
            for d in range(1, count)
        ]

    def forward_copy(h):
        return pltpu.make_async_remote_copy(
            src_ref=fwd_out.at[h],
            dst_ref=fwd_in.at[h],
            send_sem=fs_sem.at[h],
            recv_sem=fr_sem.at[h],
            device_id={"ctx": later},
            device_id_type=MESH,
        )

    def backward_copy(h):
        return pltpu.make_async_remote_copy(
            src_ref=bwd_out.at[h],
            dst_ref=bwd_in.at[h],
            send_sem=bs_sem.at[h],
            recv_sem=br_sem.at[h],
            device_id={"ctx": earlier},
            device_id_type=MESH,
        )

    row = lax.broadcasted_iota(jnp.int32, (length, HEAD_DIM), 0).astype(F32)

    def rate_of(h):
        return exp_ref[h].astype(F32) * (math.log(2.0) / (4.0 * seq_len))

    def key_decay(h):
        return jnp.exp(-rate_of(h) * (length - row))

    def query_decay(h):
        return jnp.exp(-rate_of(h) * row)

    def block_decay(h):
        return jnp.exp(jnp.full((HEAD_DIM, HEAD_DIM), -rate_of(h) * length, F32))

    def summarize(h):
        scaled = (key_decay(h) * key_v[:, columns(h)].astype(F32)).astype(LOW)
        summary = dot(scaled, value_v[:, columns(h)], 0, 0)

        @pl.when(is_first)
        def _():
            fwd_out[h] = summary
            forward_copy(h).start()

        @pl.when(jnp.logical_not(is_first))
        def _():
            local_v[h] = summary

    for copy in loads[:3]:
        copy.wait()
    loop(0, heads, summarize)
    for copy in loads[3:]:
        copy.wait()
    gain_v[...] = gain_ref[...].astype(F32)
    square_acc[...] = jnp.zeros_like(square_acc)
    dot_acc[...] = jnp.zeros_like(dot_acc)

    def attend(h):
        gap = (
            lax.broadcasted_iota(jnp.int32, (length, length), 0)
            - lax.broadcasted_iota(jnp.int32, (length, length), 1)
        ).astype(F32)
        mask = jnp.where(gap >= 0, jnp.exp(-rate_of(h) * jnp.maximum(gap, 0.0)), 0.0)
        mask_v[h] = mask
        query = query_v[:, columns(h)]
        weights = (dot(query, key_v[:, columns(h)], 1, 1) * mask).astype(LOW)
        weight_v[h] = weights
        attn_v[h] = dot(weights, value_v[:, columns(h)], 1, 0)

        @pl.when(is_first)
        def _():
            low_v[h] = jnp.zeros((HEAD_DIM, HEAD_DIM), LOW)

        @pl.when(jnp.logical_not(is_first))
        def _():
            forward_copy(h).wait_recv()

            @pl.when(jnp.logical_not(is_last))
            def _():
                fwd_out[h] = block_decay(h) * fwd_in[h] + local_v[h]
                forward_copy(h).start()

            low_v[h] = fwd_in[h].astype(LOW)

        attn = attn_v[h] + query_decay(h) * dot(query_v[:, columns(h)], low_v[h], 1, 0)
        attn_v[h] = attn
        square_acc[...] += attn * attn
        dot_acc[...] += grad_v[:, columns(h)].astype(F32) * gain_v[pl.ds(h, 1), :] * attn

    loop(0, heads, attend)

    exact = lax.Precision.HIGHEST
    ones = jnp.ones((8, HEAD_DIM), F32)
    upper = lax.broadcasted_iota(jnp.int32, (8, length), 0) < 4
    norm_mine[...] = jnp.where(
        upper, dot(ones, square_acc[...], 1, 1, exact), dot(ones, dot_acc[...], 1, 1, exact)
    )
    norm_copies = share("tensor", at_tensor, n_tensor, norm_mine, norm_in, ts_sem, tr_sem)
    for copy in norm_copies:
        copy.start()
    total = norm_mine[...]
    for d, copy in enumerate(norm_copies):
        copy.wait_recv()
        total = total + norm_in[d]
    pick = lax.broadcasted_iota(jnp.int32, (8, HEAD_DIM), 0)
    square_sum = dot(total, (pick == 0).astype(F32), 0, 0, exact)
    dot_sum = dot(total, (pick == 4).astype(F32), 0, 0, exact)
    inv_rms = lax.rsqrt(square_sum / channels + norm_eps)
    mean_dot = dot_sum / channels
    square_acc[...] = inv_rms
    dot_acc[...] = inv_rms * inv_rms * mean_dot

    def back_summary(h):
        attn = attn_v[h]
        inverse = square_acc[...]
        gain = gain_v[pl.ds(h, 1), :]
        grad = grad_v[:, columns(h)].astype(F32)
        grad_low = (inverse * (grad * gain - attn * dot_acc[...])).astype(LOW)
        gl_v[h] = grad_low
        scaled = (query_decay(h) * query_v[:, columns(h)].astype(F32)).astype(LOW)
        part = dot(scaled, grad_low, 0, 0)

        @pl.when(is_last)
        def _():
            bwd_out[h] = part
            backward_copy(h).start()

        @pl.when(jnp.logical_not(is_last))
        def _():
            local_v[h] = part

        normed = attn * inverse
        attn_out[:, columns(h)] = (gain * normed).astype(LOW)
        gpart_v[pl.ds(h, 1), :] = jnp.sum(grad * normed, axis=0, keepdims=True)

    loop(0, heads, back_summary)
    ctx_copies = share("ctx", at_ctx, n_ctx, gpart_v, ctx_in, cs_sem, cr_sem)
    for copy in ctx_copies:
        copy.start()

    def gradients(h):
        grad_low = gl_v[h]
        dweights = (dot(grad_low, value_v[:, columns(h)], 1, 1) * mask_v[h]).astype(LOW)
        query_part = dot(dweights, key_v[:, columns(h)], 1, 0)
        query_part += query_decay(h) * dot(grad_low, low_v[h], 1, 1)
        qgrad_out[:, columns(h)] = query_part.astype(LOW)
        key_part = dot(dweights, query_v[:, columns(h)], 0, 0)
        value_part = dot(weight_v[h], grad_low, 0, 0)

        @pl.when(is_last)
        def _():
            kgrad_out[:, columns(h)] = key_part.astype(LOW)
            vgrad_out[:, columns(h)] = value_part.astype(LOW)

        @pl.when(jnp.logical_not(is_last))
        def _():
            backward_copy(h).wait_recv()

            @pl.when(jnp.logical_not(is_first))
            def _():
                bwd_out[h] = block_decay(h) * bwd_in[h] + local_v[h]
                backward_copy(h).start()

            back_low = bwd_in[h].astype(LOW)
            decay = key_decay(h)
            kgrad_out[:, columns(h)] = (key_part + decay * dot(value_v[:, columns(h)], back_low, 1, 1)).astype(LOW)
            vgrad_out[:, columns(h)] = (value_part + decay * dot(key_v[:, columns(h)], back_low, 1, 0)).astype(LOW)


    third = heads // 3
    loop(0, third, gradients)
    gain_sum = gpart_v[...]
    for d, copy in enumerate(ctx_copies):
        copy.wait_recv()
        gain_sum = gain_sum + ctx_in[d]
    dp_mine[...] = gain_sum
    dp_copies = share("dp", at_dp, n_dp, dp_mine, dp_in, ds_sem, dr_sem)
    for copy in dp_copies:
        copy.start()
    loop(third, heads - 1, gradients)

    gain_sum = dp_mine[...]
    for d, copy in enumerate(dp_copies):
        copy.wait_recv()
        gain_sum = gain_sum + dp_in[d]
    width = master_ref.shape[1]
    place = (at_dp * n_ctx + at_ctx) * width
    chosen = lax.broadcasted_iota(jnp.int32, (HEAD_DIM, width), 0) == (
        lax.broadcasted_iota(jnp.int32, (HEAD_DIM, width), 1) + place
    )
    gain_grad = dot(gain_sum, chosen.astype(F32), 1, 0, exact) / math.sqrt(token_count)
    moment_new = beta_one * first_ref[...] + (1.0 - beta_one) * gain_grad
    second_new = beta_two * second_ref[...] + (1.0 - beta_two) * gain_grad * gain_grad
    moment_out[...] = moment_new
    second_out[...] = second_new
    master_out[...] = master_ref[...] - learn_rate * (moment_new / bias_one) / (
        jnp.sqrt(second_new / bias_two) + adam_eps
    )

    loop(heads - 1, heads, gradients)

    def finish(h):
        @pl.when(jnp.logical_not(is_last))
        def _():
            forward_copy(h).wait_send()

        @pl.when(jnp.logical_not(is_first))
        def _():
            backward_copy(h).wait_send()

    loop(0, heads, finish)
    for copy in norm_copies + ctx_copies + dp_copies:
        copy.wait_send()


def store_all(*refs):
    sems = refs[14]
    copies = [
        pltpu.make_async_copy(source, target, sems.at[i])
        for i, (source, target) in enumerate(zip(refs[:7], refs[7:14]))
    ]
    for copy in copies:
        copy.start()
    for copy in copies:
        copy.wait()


def body(
    mesh_dims,
    query_rows,
    key_rows,
    value_rows,
    decay_exp,
    out_grad,
    gain_weight,
    master_gain,
    first_moment,
    second_moment,
):
    _, length, row_width = query_rows.shape
    heads = row_width // HEAD_DIM
    n_dp, n_ctx, n_tensor = mesh_dims
    rows = (length, row_width)
    tile = (heads, length, HEAD_DIM)
    state = (heads, HEAD_DIM, HEAD_DIM)
    gain_dims = (heads, HEAD_DIM)
    hbm_spec = pl.BlockSpec(memory_space=pltpu.HBM)
    vmem_spec = pl.BlockSpec(memory_space=pltpu.VMEM)
    dma = pltpu.SemaphoreType.DMA
    scratch = (
        [pltpu.SMEM((heads,), jnp.int32)]
        + [pltpu.VMEM(rows, LOW)] * 4
        + [pltpu.VMEM(gain_dims, LOW)]
        + [pltpu.VMEM(master_gain.shape, F32)] * 3
        + [
            pltpu.VMEM(tile, F32),
            pltpu.VMEM((heads, length, length), F32),
            pltpu.VMEM((heads, length, length), LOW),
            pltpu.VMEM(state, LOW),
        ]
        + [pltpu.VMEM(state, F32)] * 5
        + [
            pltpu.VMEM(tile, LOW),
            pltpu.VMEM(gain_dims, F32),
            pltpu.VMEM(gain_dims, F32),
            pltpu.VMEM((length, HEAD_DIM), F32),
            pltpu.VMEM((length, HEAD_DIM), F32),
            pltpu.VMEM((8, length), F32),
            pltpu.VMEM((n_tensor - 1, 8, length), F32),
            pltpu.VMEM((n_ctx - 1,) + gain_dims, F32),
            pltpu.VMEM(gain_dims, F32),
            pltpu.VMEM((n_dp - 1,) + gain_dims, F32),
            dma((9,)),
        ]
        + [dma((heads,))] * 4
        + [dma((count - 1,)) for count in (n_tensor, n_tensor, n_ctx, n_ctx, n_dp, n_dp)]
    )
    out_shape = [jax.ShapeDtypeStruct(rows, LOW)] * 4 + [
        jax.ShapeDtypeStruct(master_gain.shape, F32)
    ] * 3
    held = pl.pallas_call(
        functools.partial(fused, (heads, length, n_dp, n_ctx, n_tensor)),
        out_shape=out_shape,
        in_specs=[hbm_spec] * 9,
        out_specs=[vmem_spec] * 7,
        scratch_shapes=scratch,
        compiler_params=pltpu.CompilerParams(
            collective_id=0, has_side_effects=True, vmem_limit_bytes=67043328
        ),
        name="fused",
    )(
        decay_exp,
        query_rows.reshape(rows),
        key_rows.reshape(rows),
        value_rows.reshape(rows),
        out_grad.reshape(rows),
        gain_weight,
        master_gain,
        first_moment,
        second_moment,
    )
    results = pl.pallas_call(
        store_all,
        out_shape=out_shape,
        in_specs=[vmem_spec] * 7,
        out_specs=[hbm_spec] * 7,
        scratch_shapes=[dma((7,))],
        name="store_all",
    )(*held)
    full = tuple(part.reshape(query_rows.shape) for part in results[:4])
    return full + tuple(results[4:])


def solution(mesh):
    rows = P("dp", "ctx", "tensor")
    share = P("tensor", ("dp", "ctx"))
    mesh_dims = (mesh.shape["dp"], mesh.shape["ctx"], mesh.shape["tensor"])
    return jax.shard_map(
        functools.partial(body, mesh_dims),
        mesh=mesh,
        in_specs=(rows, rows, rows, P("tensor"), rows, P("tensor", None), share, share, share),
        out_specs=(rows, rows, rows, rows, share, share, share),
        check_vma=False,
    )
```

```python
import functools
import math

import jax
import jax.numpy as jnp
from jax import lax
from jax.experimental import pallas as pl
from jax.experimental.pallas import tpu as pltpu
from jax.sharding import PartitionSpec as P

HEAD_DIM = 128
PARTS = 2
MESH = pl.DeviceIdType.MESH

beta_one = 0.9
beta_two = 0.95
learn_rate = 0.02
adam_eps = 1e-08
bias_one = 0.9999734386011124
bias_two = 0.9940794707796667
norm_eps = 1e-05

LOW = jnp.bfloat16
F32 = jnp.float32


def dot(a, b, dim_a, dim_b, precision=None):
    return lax.dot_general(
        a, b, (((dim_a,), (dim_b,)), ((), ())), preferred_element_type=F32, precision=precision
    )


def fused(
    dims,
    exp_hbm,
    query_hbm,
    key_hbm,
    value_hbm,
    grad_hbm,
    gain_hbm,
    master_hbm,
    first_hbm,
    second_hbm,
    attn_hbm,
    qgrad_hbm,
    kgrad_hbm,
    vgrad_hbm,
    master_out,
    moment_out,
    second_out,
    attn_out,
    qgrad_out,
    kgrad_out,
    vgrad_out,
    exp_ref,
    query_v,
    key_v,
    value_v,
    grad_v,
    gain_ref,
    master_ref,
    first_ref,
    second_ref,
    attn_v,
    mask_v,
    weight_v,
    low_v,
    local_v,
    fwd_in,
    fwd_out,
    bwd_in,
    bwd_out,
    gl_v,
    gain_v,
    gpart_v,
    square_acc,
    dot_acc,
    norm_mine,
    norm_in,
    ctx_in,
    dp_mine,
    dp_in,
    in_sem,
    attn_sem,
    out_sem,
    fs_sem,
    fr_sem,
    bs_sem,
    br_sem,
    ts_sem,
    tr_sem,
    cs_sem,
    cr_sem,
    ds_sem,
    dr_sem,
):
    heads, length, n_dp, n_ctx, n_tensor = dims
    seq_len = length * n_ctx
    channels = heads * HEAD_DIM * n_tensor
    token_count = n_dp * seq_len
    at_dp, at_ctx, at_tensor = (lax.axis_index(name) for name in ("dp", "ctx", "tensor"))
    later = lax.rem(at_ctx + 1, n_ctx)
    earlier = lax.rem(at_ctx + n_ctx - 1, n_ctx)
    is_first, is_last = at_ctx == 0, at_ctx == n_ctx - 1

    def columns(h):
        return pl.ds(pl.multiple_of(h * HEAD_DIM, HEAD_DIM), HEAD_DIM)

    pairs = (
        (exp_hbm, exp_ref),
        (key_hbm, key_v),
        (value_hbm, value_v),
        (query_hbm, query_v),
        (grad_hbm, grad_v),
        (gain_hbm, gain_ref),
        (master_hbm, master_ref),
        (first_hbm, first_ref),
        (second_hbm, second_ref),
    )
    loads = [
        pltpu.make_async_copy(hbm, local, in_sem.at[i]) for i, (hbm, local) in enumerate(pairs)
    ]
    def loop(low, high, step):
        lax.fori_loop(low, high, lambda h, c: (step(h), c)[1], 0)

    attn_save = pltpu.make_async_copy(attn_out, attn_hbm, attn_sem.at[0])
    outs = ((qgrad_out, qgrad_hbm), (kgrad_out, kgrad_hbm), (vgrad_out, vgrad_hbm))

    def save(which, h):
        local, hbm = outs[which]
        return pltpu.make_async_copy(
            local.at[:, columns(h)], hbm.at[:, columns(h)], out_sem.at[which, h]
        )

    barrier = pltpu.get_barrier_semaphore()
    groups = (("dp", at_dp, n_dp), ("ctx", at_ctx, n_ctx), ("tensor", at_tensor, n_tensor))
    for name, mine, count in groups:
        for d in range(1, count):
            pl.semaphore_signal(
                barrier, inc=1, device_id={name: lax.rem(mine + d, count)}, device_id_type=MESH
            )
    for copy in loads:
        copy.start()

    def share(name, mine, count, source, slots, send_sem, recv_sem):
        return [
            pltpu.make_async_remote_copy(
                src_ref=source,
                dst_ref=slots.at[d - 1],
                send_sem=send_sem.at[d - 1],
                recv_sem=recv_sem.at[d - 1],
                device_id={name: lax.rem(mine + d, count)},
                device_id_type=MESH,
            )
            for d in range(1, count)
        ]

    part_rows = HEAD_DIM // PARTS

    def some_rows(part):
        return pl.ds(part * part_rows, part_rows)

    def forward_copy(h, part):
        return pltpu.make_async_remote_copy(
            src_ref=fwd_out.at[h, some_rows(part)],
            dst_ref=fwd_in.at[h, some_rows(part)],
            send_sem=fs_sem.at[h, part],
            recv_sem=fr_sem.at[h, part],
            device_id={"ctx": later},
            device_id_type=MESH,
        )

    def backward_copy(h, part):
        return pltpu.make_async_remote_copy(
            src_ref=bwd_out.at[h, some_rows(part)],
            dst_ref=bwd_in.at[h, some_rows(part)],
            send_sem=bs_sem.at[h, part],
            recv_sem=br_sem.at[h, part],
            device_id={"ctx": earlier},
            device_id_type=MESH,
        )

    row = lax.broadcasted_iota(jnp.int32, (length, HEAD_DIM), 0).astype(F32)

    def rate_of(h):
        return exp_ref[h].astype(F32) * (math.log(2.0) / (4.0 * seq_len))

    def key_decay(h):
        return jnp.exp(-rate_of(h) * (length - row))

    def query_decay(h):
        return jnp.exp(-rate_of(h) * row)

    def block_decay(h):
        return jnp.exp(jnp.full((part_rows, HEAD_DIM), -rate_of(h) * length, F32))

    def summarize(h):
        scaled = (key_decay(h) * key_v[:, columns(h)].astype(F32)).astype(LOW)
        summary = dot(scaled, value_v[:, columns(h)], 0, 0)

        @pl.when(is_first)
        def _():
            fwd_out[h] = summary

        @pl.when(jnp.logical_not(is_first))
        def _():
            local_v[h] = summary

    for copy in loads[:3]:
        copy.wait()
    loop(0, heads, summarize)
    pl.semaphore_wait(barrier, n_dp + n_ctx + n_tensor - 3)

    @pl.when(is_first)
    def _():
        def send(h):
            for part in range(PARTS):
                forward_copy(h, part).start()

        loop(0, heads, send)

    for copy in loads[3:]:
        copy.wait()
    gain_v[...] = gain_ref[...].astype(F32)
    square_acc[...] = jnp.zeros_like(square_acc)
    dot_acc[...] = jnp.zeros_like(dot_acc)

    def attend(h):
        gap = (
            lax.broadcasted_iota(jnp.int32, (length, length), 0)
            - lax.broadcasted_iota(jnp.int32, (length, length), 1)
        ).astype(F32)
        mask = jnp.where(gap >= 0, jnp.exp(-rate_of(h) * jnp.maximum(gap, 0.0)), 0.0)
        mask_v[h] = mask
        query = query_v[:, columns(h)]
        weights = (dot(query, key_v[:, columns(h)], 1, 1) * mask).astype(LOW)
        weight_v[h] = weights
        attn_v[h] = dot(weights, value_v[:, columns(h)], 1, 0)

        @pl.when(is_first)
        def _():
            low_v[h] = jnp.zeros((HEAD_DIM, HEAD_DIM), LOW)

        @pl.when(jnp.logical_not(is_first))
        def _():
            for part in range(PARTS):
                rows = some_rows(part)
                forward_copy(h, part).wait_recv()

                @pl.when(jnp.logical_not(is_last))
                def _():
                    fwd_out[h, rows] = block_decay(h) * fwd_in[h, rows] + local_v[h, rows]
                    forward_copy(h, part).start()

            low_v[h] = fwd_in[h].astype(LOW)

        attn = attn_v[h] + query_decay(h) * dot(query_v[:, columns(h)], low_v[h], 1, 0)
        attn_v[h] = attn
        square_acc[...] += attn * attn
        dot_acc[...] += grad_v[:, columns(h)].astype(F32) * gain_v[pl.ds(h, 1), :] * attn

    loop(0, heads, attend)

    exact = lax.Precision.HIGHEST
    ones = jnp.ones((8, HEAD_DIM), F32)
    upper = lax.broadcasted_iota(jnp.int32, (8, length), 0) < 4
    norm_mine[...] = jnp.where(
        upper, dot(ones, square_acc[...], 1, 1, exact), dot(ones, dot_acc[...], 1, 1, exact)
    )
    norm_copies = share("tensor", at_tensor, n_tensor, norm_mine, norm_in, ts_sem, tr_sem)
    for copy in norm_copies:
        copy.start()
    total = norm_mine[...]
    for d, copy in enumerate(norm_copies):
        copy.wait_recv()
        total = total + norm_in[d]
    pick = lax.broadcasted_iota(jnp.int32, (8, HEAD_DIM), 0)
    square_sum = dot(total, (pick == 0).astype(F32), 0, 0, exact)
    dot_sum = dot(total, (pick == 4).astype(F32), 0, 0, exact)
    inv_rms = lax.rsqrt(square_sum / channels + norm_eps)
    mean_dot = dot_sum / channels
    square_acc[...] = inv_rms
    dot_acc[...] = inv_rms * inv_rms * mean_dot

    def back_summary(h):
        attn = attn_v[h]
        inverse = square_acc[...]
        gain = gain_v[pl.ds(h, 1), :]
        grad = grad_v[:, columns(h)].astype(F32)
        grad_low = (inverse * (grad * gain - attn * dot_acc[...])).astype(LOW)
        gl_v[h] = grad_low
        scaled = (query_decay(h) * query_v[:, columns(h)].astype(F32)).astype(LOW)
        part = dot(scaled, grad_low, 0, 0)

        @pl.when(is_last)
        def _():
            bwd_out[h] = part
            for piece in range(PARTS):
                backward_copy(h, piece).start()

        @pl.when(jnp.logical_not(is_last))
        def _():
            local_v[h] = part

        normed = attn * inverse
        attn_out[:, columns(h)] = (gain * normed).astype(LOW)
        gpart_v[pl.ds(h, 1), :] = jnp.sum(grad * normed, axis=0, keepdims=True)

    loop(0, heads, back_summary)
    attn_save.start()
    ctx_copies = share("ctx", at_ctx, n_ctx, gpart_v, ctx_in, cs_sem, cr_sem)
    for copy in ctx_copies:
        copy.start()

    def gradients(h):
        grad_low = gl_v[h]
        dweights = (dot(grad_low, value_v[:, columns(h)], 1, 1) * mask_v[h]).astype(LOW)
        query_part = dot(dweights, key_v[:, columns(h)], 1, 0)
        query_part += query_decay(h) * dot(grad_low, low_v[h], 1, 1)
        qgrad_out[:, columns(h)] = query_part.astype(LOW)
        key_part = dot(dweights, query_v[:, columns(h)], 0, 0)
        value_part = dot(weight_v[h], grad_low, 0, 0)

        @pl.when(is_last)
        def _():
            kgrad_out[:, columns(h)] = key_part.astype(LOW)
            vgrad_out[:, columns(h)] = value_part.astype(LOW)

        @pl.when(jnp.logical_not(is_last))
        def _():
            for part in range(PARTS):
                rows = some_rows(part)
                backward_copy(h, part).wait_recv()

                @pl.when(jnp.logical_not(is_first))
                def _():
                    bwd_out[h, rows] = block_decay(h) * bwd_in[h, rows] + local_v[h, rows]
                    backward_copy(h, part).start()

            back_low = bwd_in[h].astype(LOW)
            decay = key_decay(h)
            kgrad_out[:, columns(h)] = (key_part + decay * dot(value_v[:, columns(h)], back_low, 1, 1)).astype(LOW)
            vgrad_out[:, columns(h)] = (value_part + decay * dot(key_v[:, columns(h)], back_low, 1, 0)).astype(LOW)

        for which in range(3):
            save(which, h).start()


    loop(0, heads - 2, gradients)
    gain_sum = gpart_v[...]
    for d, copy in enumerate(ctx_copies):
        copy.wait_recv()
        gain_sum = gain_sum + ctx_in[d]
    dp_mine[...] = gain_sum
    dp_copies = share("dp", at_dp, n_dp, dp_mine, dp_in, ds_sem, dr_sem)
    for copy in dp_copies:
        copy.start()
    loop(heads - 2, heads, gradients)

    gain_sum = dp_mine[...]
    for d, copy in enumerate(dp_copies):
        copy.wait_recv()
        gain_sum = gain_sum + dp_in[d]
    width = master_ref.shape[1]
    place = (at_dp * n_ctx + at_ctx) * width
    chosen = lax.broadcasted_iota(jnp.int32, (HEAD_DIM, width), 0) == (
        lax.broadcasted_iota(jnp.int32, (HEAD_DIM, width), 1) + place
    )
    gain_grad = dot(gain_sum, chosen.astype(F32), 1, 0, exact) / math.sqrt(token_count)
    moment_new = beta_one * first_ref[...] + (1.0 - beta_one) * gain_grad
    second_new = beta_two * second_ref[...] + (1.0 - beta_two) * gain_grad * gain_grad
    moment_out[...] = moment_new
    second_out[...] = second_new
    master_out[...] = master_ref[...] - learn_rate * (moment_new / bias_one) / (
        jnp.sqrt(second_new / bias_two) + adam_eps
    )

    attn_save.wait()

    def finish(h):
        for which in range(3):
            save(which, h).wait()

        @pl.when(jnp.logical_not(is_last))
        def _():
            for part in range(PARTS):
                forward_copy(h, part).wait_send()

        @pl.when(jnp.logical_not(is_first))
        def _():
            for part in range(PARTS):
                backward_copy(h, part).wait_send()

    loop(0, heads, finish)
    for copy in norm_copies + ctx_copies + dp_copies:
        copy.wait_send()


def store_all(*refs):
    count = len(refs) // 3
    sources, targets, held = refs[:count], refs[count : 2 * count], refs[2 * count : 3 * count]
    sems = refs[3 * count]
    reads = [
        pltpu.make_async_copy(source, local, sems.at[0, i])
        for i, (source, local) in enumerate(zip(sources, held))
    ]
    writes = [
        pltpu.make_async_copy(local, target, sems.at[1, i])
        for i, (target, local) in enumerate(zip(targets, held))
    ]
    for copy in reads:
        copy.start()
    for read, write in zip(reads, writes):
        read.wait()
        write.start()
    for copy in writes:
        copy.wait()


def body(
    mesh_dims,
    query_rows,
    key_rows,
    value_rows,
    decay_exp,
    out_grad,
    gain_weight,
    master_gain,
    first_moment,
    second_moment,
):
    _, length, row_width = query_rows.shape
    heads = row_width // HEAD_DIM
    n_dp, n_ctx, n_tensor = mesh_dims
    rows = (length, row_width)
    tile = (heads, length, HEAD_DIM)
    state = (heads, HEAD_DIM, HEAD_DIM)
    gain_dims = (heads, HEAD_DIM)
    hbm_spec = pl.BlockSpec(memory_space=pltpu.HBM)
    vmem_spec = pl.BlockSpec(memory_space=pltpu.VMEM)
    dma = pltpu.SemaphoreType.DMA
    scratch = (
        [pltpu.VMEM(rows, LOW)] * 4
        + [pltpu.SMEM((heads,), jnp.int32)]
        + [pltpu.VMEM(rows, LOW)] * 4
        + [pltpu.VMEM(gain_dims, LOW)]
        + [pltpu.VMEM(master_gain.shape, F32)] * 3
        + [
            pltpu.VMEM(tile, F32),
            pltpu.VMEM((heads, length, length), F32),
            pltpu.VMEM((heads, length, length), LOW),
            pltpu.VMEM(state, LOW),
        ]
        + [pltpu.VMEM(state, F32)] * 5
        + [
            pltpu.VMEM(tile, LOW),
            pltpu.VMEM(gain_dims, F32),
            pltpu.VMEM(gain_dims, F32),
            pltpu.VMEM((length, HEAD_DIM), F32),
            pltpu.VMEM((length, HEAD_DIM), F32),
            pltpu.VMEM((8, length), F32),
            pltpu.VMEM((n_tensor - 1, 8, length), F32),
            pltpu.VMEM((n_ctx - 1,) + gain_dims, F32),
            pltpu.VMEM(gain_dims, F32),
            pltpu.VMEM((n_dp - 1,) + gain_dims, F32),
            dma((9,)),
            dma((1,)),
            dma((3, heads)),
        ]
        + [dma((heads, PARTS))] * 4
        + [dma((count - 1,)) for count in (n_tensor, n_tensor, n_ctx, n_ctx, n_dp, n_dp)]
    )
    out_shape = [jax.ShapeDtypeStruct(rows, LOW)] * 4 + [
        jax.ShapeDtypeStruct(master_gain.shape, F32)
    ] * 3
    held = pl.pallas_call(
        functools.partial(fused, (heads, length, n_dp, n_ctx, n_tensor)),
        out_shape=out_shape,
        in_specs=[hbm_spec] * 9,
        out_specs=[hbm_spec] * 4 + [vmem_spec] * 3,
        scratch_shapes=scratch,
        compiler_params=pltpu.CompilerParams(
            collective_id=0, has_side_effects=True, vmem_limit_bytes=67043328
        ),
        name="fused",
    )(
        decay_exp,
        query_rows.reshape(rows),
        key_rows.reshape(rows),
        value_rows.reshape(rows),
        out_grad.reshape(rows),
        gain_weight,
        master_gain,
        first_moment,
        second_moment,
    )
    results = pl.pallas_call(
        store_all,
        out_shape=out_shape,
        in_specs=[hbm_spec] * 7,
        out_specs=[hbm_spec] * 7,
        scratch_shapes=[pltpu.VMEM(part.shape, part.dtype) for part in out_shape] + [dma((2, 7))],
        compiler_params=pltpu.CompilerParams(vmem_limit_bytes=67043328),
        name="store_all",
    )(*held)
    full = tuple(part.reshape(query_rows.shape) for part in results[:4])
    return full + tuple(results[4:])


def solution(mesh):
    rows = P("dp", "ctx", "tensor")
    share = P("tensor", ("dp", "ctx"))
    mesh_dims = (mesh.shape["dp"], mesh.shape["ctx"], mesh.shape["tensor"])
    return jax.shard_map(
        functools.partial(body, mesh_dims),
        mesh=mesh,
        in_specs=(rows, rows, rows, P("tensor"), rows, P("tensor", None), share, share, share),
        out_specs=(rows, rows, rows, rows, share, share, share),
        check_vma=False,
    )
```

```python
import functools
import math

import jax
import jax.numpy as jnp
from jax import lax
from jax.experimental import pallas as pl
from jax.experimental.pallas import tpu as pltpu
from jax.sharding import PartitionSpec as P

HEAD_DIM = 128
PARTS = 2
MESH = pl.DeviceIdType.MESH

beta_one = 0.9
beta_two = 0.95
learn_rate = 0.02
adam_eps = 1e-08
bias_one = 0.9999734386011124
bias_two = 0.9940794707796667
norm_eps = 1e-05

LOW = jnp.bfloat16
F32 = jnp.float32


def dot(a, b, dim_a, dim_b, precision=None):
    return lax.dot_general(
        a, b, (((dim_a,), (dim_b,)), ((), ())), preferred_element_type=F32, precision=precision
    )


def fused(
    dims,
    exp_hbm,
    query_hbm,
    key_hbm,
    value_hbm,
    grad_hbm,
    gain_hbm,
    master_hbm,
    first_hbm,
    second_hbm,
    attn_hbm,
    qgrad_hbm,
    kgrad_hbm,
    vgrad_hbm,
    master_out,
    moment_out,
    second_out,
    attn_out,
    qgrad_out,
    kgrad_out,
    vgrad_out,
    exp_ref,
    query_v,
    key_v,
    value_v,
    grad_v,
    gain_ref,
    master_ref,
    first_ref,
    second_ref,
    attn_v,
    mask_v,
    weight_v,
    low_v,
    local_v,
    fwd_in,
    fwd_out,
    bwd_in,
    bwd_out,
    gl_v,
    gain_v,
    gpart_v,
    square_acc,
    dot_acc,
    norm_mine,
    norm_in,
    ctx_in,
    dp_mine,
    dp_in,
    in_sem,
    attn_sem,
    out_sem,
    fs_sem,
    fr_sem,
    bs_sem,
    br_sem,
    ts_sem,
    tr_sem,
    cs_sem,
    cr_sem,
    ds_sem,
    dr_sem,
):
    heads, length, n_dp, n_ctx, n_tensor = dims
    seq_len = length * n_ctx
    channels = heads * HEAD_DIM * n_tensor
    token_count = n_dp * seq_len
    at_dp, at_ctx, at_tensor = (lax.axis_index(name) for name in ("dp", "ctx", "tensor"))
    later = lax.rem(at_ctx + 1, n_ctx)
    earlier = lax.rem(at_ctx + n_ctx - 1, n_ctx)
    is_first, is_last = at_ctx == 0, at_ctx == n_ctx - 1

    def columns(h):
        return pl.ds(pl.multiple_of(h * HEAD_DIM, HEAD_DIM), HEAD_DIM)

    pairs = (
        (exp_hbm, exp_ref),
        (key_hbm, key_v),
        (value_hbm, value_v),
        (query_hbm, query_v),
        (grad_hbm, grad_v),
        (gain_hbm, gain_ref),
        (master_hbm, master_ref),
        (first_hbm, first_ref),
        (second_hbm, second_ref),
    )
    loads = [
        pltpu.make_async_copy(hbm, local, in_sem.at[i]) for i, (hbm, local) in enumerate(pairs)
    ]
    def loop(low, high, step):
        lax.fori_loop(low, high, lambda h, c: (step(h), c)[1], 0)

    attn_save = pltpu.make_async_copy(attn_out, attn_hbm, attn_sem.at[0])
    outs = ((qgrad_out, qgrad_hbm), (kgrad_out, kgrad_hbm), (vgrad_out, vgrad_hbm))

    def save(which, h):
        local, hbm = outs[which]
        return pltpu.make_async_copy(
            local.at[:, columns(h)], hbm.at[:, columns(h)], out_sem.at[which, h]
        )

    barrier = pltpu.get_barrier_semaphore()
    groups = (("dp", at_dp, n_dp), ("ctx", at_ctx, n_ctx), ("tensor", at_tensor, n_tensor))
    for name, mine, count in groups:
        for d in range(1, count):
            pl.semaphore_signal(
                barrier, inc=1, device_id={name: lax.rem(mine + d, count)}, device_id_type=MESH
            )
    for copy in loads:
        copy.start()

    def share(name, mine, count, source, slots, send_sem, recv_sem):
        return [
            pltpu.make_async_remote_copy(
                src_ref=source,
                dst_ref=slots.at[d - 1],
                send_sem=send_sem.at[d - 1],
                recv_sem=recv_sem.at[d - 1],
                device_id={name: lax.rem(mine + d, count)},
                device_id_type=MESH,
            )
            for d in range(1, count)
        ]

    part_rows = HEAD_DIM // PARTS

    def some_rows(part):
        return pl.ds(part * part_rows, part_rows)

    def forward_copy(h, part):
        return pltpu.make_async_remote_copy(
            src_ref=fwd_out.at[h, some_rows(part)],
            dst_ref=fwd_in.at[h, some_rows(part)],
            send_sem=fs_sem.at[h, part],
            recv_sem=fr_sem.at[h, part],
            device_id={"ctx": later},
            device_id_type=MESH,
        )

    def backward_copy(h, part):
        return pltpu.make_async_remote_copy(
            src_ref=bwd_out.at[h, some_rows(part)],
            dst_ref=bwd_in.at[h, some_rows(part)],
            send_sem=bs_sem.at[h, part],
            recv_sem=br_sem.at[h, part],
            device_id={"ctx": earlier},
            device_id_type=MESH,
        )

    row = lax.broadcasted_iota(jnp.int32, (length, HEAD_DIM), 0).astype(F32)

    def rate_of(h):
        return exp_ref[h].astype(F32) * (math.log(2.0) / (4.0 * seq_len))

    def key_decay(h):
        return jnp.exp(-rate_of(h) * (length - row))

    def query_decay(h):
        return jnp.exp(-rate_of(h) * row)

    def block_decay(h):
        return jnp.exp(jnp.full((part_rows, HEAD_DIM), -rate_of(h) * length, F32))

    def summarize(h):
        scaled = (key_decay(h) * key_v[:, columns(h)].astype(F32)).astype(LOW)
        summary = dot(scaled, value_v[:, columns(h)], 0, 0)

        @pl.when(is_first)
        def _():
            fwd_out[h] = summary

        @pl.when(jnp.logical_not(is_first))
        def _():
            local_v[h] = summary

    for copy in loads[:3]:
        copy.wait()
    loop(0, heads, summarize)
    pl.semaphore_wait(barrier, n_dp + n_ctx + n_tensor - 3)

    @pl.when(is_first)
    def _():
        def send(h):
            for part in range(PARTS):
                forward_copy(h, part).start()

        loop(0, heads, send)

    for copy in loads[3:]:
        copy.wait()
    gain_v[...] = gain_ref[...].astype(F32)
    square_acc[...] = jnp.zeros_like(square_acc)
    dot_acc[...] = jnp.zeros_like(dot_acc)

    def attend(h):
        gap = (
            lax.broadcasted_iota(jnp.int32, (length, length), 0)
            - lax.broadcasted_iota(jnp.int32, (length, length), 1)
        ).astype(F32)
        mask = jnp.where(gap >= 0, jnp.exp(-rate_of(h) * jnp.maximum(gap, 0.0)), 0.0)
        mask_v[h] = mask
        query = query_v[:, columns(h)]
        weights = (dot(query, key_v[:, columns(h)], 1, 1) * mask).astype(LOW)
        weight_v[h] = weights
        attn_v[h] = dot(weights, value_v[:, columns(h)], 1, 0)

        @pl.when(is_first)
        def _():
            low_v[h] = jnp.zeros((HEAD_DIM, HEAD_DIM), LOW)

        @pl.when(jnp.logical_not(is_first))
        def _():
            for part in range(PARTS):
                rows = some_rows(part)
                forward_copy(h, part).wait_recv()

                @pl.when(jnp.logical_not(is_last))
                def _():
                    fwd_out[h, rows] = block_decay(h) * fwd_in[h, rows] + local_v[h, rows]
                    forward_copy(h, part).start()

            low_v[h] = fwd_in[h].astype(LOW)

        attn = attn_v[h] + query_decay(h) * dot(query_v[:, columns(h)], low_v[h], 1, 0)
        attn_v[h] = attn
        square_acc[...] += attn * attn
        dot_acc[...] += grad_v[:, columns(h)].astype(F32) * gain_v[pl.ds(h, 1), :] * attn

    loop(0, heads, attend)

    exact = lax.Precision.HIGHEST
    ones = jnp.ones((8, HEAD_DIM), F32)
    upper = lax.broadcasted_iota(jnp.int32, (8, length), 0) < 4
    norm_mine[...] = jnp.where(
        upper, dot(ones, square_acc[...], 1, 1, exact), dot(ones, dot_acc[...], 1, 1, exact)
    )
    norm_copies = share("tensor", at_tensor, n_tensor, norm_mine, norm_in, ts_sem, tr_sem)
    for copy in norm_copies:
        copy.start()
    total = norm_mine[...]
    for d, copy in enumerate(norm_copies):
        copy.wait_recv()
        total = total + norm_in[d]
    pick = lax.broadcasted_iota(jnp.int32, (8, HEAD_DIM), 0)
    square_sum = dot(total, (pick == 0).astype(F32), 0, 0, exact)
    dot_sum = dot(total, (pick == 4).astype(F32), 0, 0, exact)
    inv_rms = lax.rsqrt(square_sum / channels + norm_eps)
    mean_dot = dot_sum / channels
    square_acc[...] = inv_rms
    dot_acc[...] = inv_rms * inv_rms * mean_dot

    early = min(3, heads)

    def back_summary(h):
        attn = attn_v[h]
        inverse = square_acc[...]
        gain = gain_v[pl.ds(h, 1), :]
        grad = grad_v[:, columns(h)].astype(F32)
        grad_low = (inverse * (grad * gain - attn * dot_acc[...])).astype(LOW)
        gl_v[h] = grad_low
        scaled = (query_decay(h) * query_v[:, columns(h)].astype(F32)).astype(LOW)
        part = dot(scaled, grad_low, 0, 0)

        @pl.when(is_last)
        def _():
            bwd_out[h] = part

            @pl.when(h < early)
            def _():
                for piece in range(PARTS):
                    backward_copy(h, piece).start()

        @pl.when(jnp.logical_not(is_last))
        def _():
            local_v[h] = part

        normed = attn * inverse
        attn_out[:, columns(h)] = (gain * normed).astype(LOW)
        gpart_v[pl.ds(h, 1), :] = jnp.sum(grad * normed, axis=0, keepdims=True)

    loop(0, heads, back_summary)
    ctx_copies = share("ctx", at_ctx, n_ctx, gpart_v, ctx_in, cs_sem, cr_sem)
    for copy in ctx_copies:
        copy.start()

    @pl.when(is_last)
    def _():
        def send(h):
            for part in range(PARTS):
                backward_copy(h, part).start()

        loop(early, heads, send)


    attn_save.start()

    def gradients(h):
        grad_low = gl_v[h]
        dweights = (dot(grad_low, value_v[:, columns(h)], 1, 1) * mask_v[h]).astype(LOW)
        query_part = dot(dweights, key_v[:, columns(h)], 1, 0)
        query_part += query_decay(h) * dot(grad_low, low_v[h], 1, 1)
        qgrad_out[:, columns(h)] = query_part.astype(LOW)
        key_part = dot(dweights, query_v[:, columns(h)], 0, 0)
        value_part = dot(weight_v[h], grad_low, 0, 0)

        @pl.when(is_last)
        def _():
            kgrad_out[:, columns(h)] = key_part.astype(LOW)
            vgrad_out[:, columns(h)] = value_part.astype(LOW)

        @pl.when(jnp.logical_not(is_last))
        def _():
            for part in range(PARTS):
                rows = some_rows(part)
                backward_copy(h, part).wait_recv()

                @pl.when(jnp.logical_not(is_first))
                def _():
                    bwd_out[h, rows] = block_decay(h) * bwd_in[h, rows] + local_v[h, rows]
                    backward_copy(h, part).start()

            back_low = bwd_in[h].astype(LOW)
            decay = key_decay(h)
            kgrad_out[:, columns(h)] = (key_part + decay * dot(value_v[:, columns(h)], back_low, 1, 1)).astype(LOW)
            vgrad_out[:, columns(h)] = (value_part + decay * dot(key_v[:, columns(h)], back_low, 1, 0)).astype(LOW)

        for which in range(3):
            save(which, h).start()


    loop(0, heads - 2, gradients)
    gain_sum = gpart_v[...]
    for d, copy in enumerate(ctx_copies):
        copy.wait_recv()
        gain_sum = gain_sum + ctx_in[d]
    dp_mine[...] = gain_sum
    dp_copies = share("dp", at_dp, n_dp, dp_mine, dp_in, ds_sem, dr_sem)
    for copy in dp_copies:
        copy.start()
    loop(heads - 2, heads, gradients)

    gain_sum = dp_mine[...]
    for d, copy in enumerate(dp_copies):
        copy.wait_recv()
        gain_sum = gain_sum + dp_in[d]
    width = master_ref.shape[1]
    place = (at_dp * n_ctx + at_ctx) * width
    chosen = lax.broadcasted_iota(jnp.int32, (HEAD_DIM, width), 0) == (
        lax.broadcasted_iota(jnp.int32, (HEAD_DIM, width), 1) + place
    )
    gain_grad = dot(gain_sum, chosen.astype(F32), 1, 0, exact) / math.sqrt(token_count)
    moment_new = beta_one * first_ref[...] + (1.0 - beta_one) * gain_grad
    second_new = beta_two * second_ref[...] + (1.0 - beta_two) * gain_grad * gain_grad
    moment_out[...] = moment_new
    second_out[...] = second_new
    master_out[...] = master_ref[...] - learn_rate * (moment_new / bias_one) / (
        jnp.sqrt(second_new / bias_two) + adam_eps
    )

    attn_save.wait()

    def finish(h):
        for which in range(3):
            save(which, h).wait()

        @pl.when(jnp.logical_not(is_last))
        def _():
            for part in range(PARTS):
                forward_copy(h, part).wait_send()

        @pl.when(jnp.logical_not(is_first))
        def _():
            for part in range(PARTS):
                backward_copy(h, part).wait_send()

    loop(0, heads, finish)
    for copy in norm_copies + ctx_copies + dp_copies:
        copy.wait_send()


def store_all(*refs):
    count = len(refs) // 3
    sources, targets, held = refs[:count], refs[count : 2 * count], refs[2 * count : 3 * count]
    sems = refs[3 * count]
    reads = [
        pltpu.make_async_copy(source, local, sems.at[0, i])
        for i, (source, local) in enumerate(zip(sources, held))
    ]
    writes = [
        pltpu.make_async_copy(local, target, sems.at[1, i])
        for i, (target, local) in enumerate(zip(targets, held))
    ]
    for copy in reads:
        copy.start()
    for read, write in zip(reads, writes):
        read.wait()
        write.start()
    for copy in writes:
        copy.wait()


def body(
    mesh_dims,
    query_rows,
    key_rows,
    value_rows,
    decay_exp,
    out_grad,
    gain_weight,
    master_gain,
    first_moment,
    second_moment,
):
    _, length, row_width = query_rows.shape
    heads = row_width // HEAD_DIM
    n_dp, n_ctx, n_tensor = mesh_dims
    rows = (length, row_width)
    tile = (heads, length, HEAD_DIM)
    state = (heads, HEAD_DIM, HEAD_DIM)
    gain_dims = (heads, HEAD_DIM)
    hbm_spec = pl.BlockSpec(memory_space=pltpu.HBM)
    vmem_spec = pl.BlockSpec(memory_space=pltpu.VMEM)
    dma = pltpu.SemaphoreType.DMA
    scratch = (
        [pltpu.VMEM(rows, LOW)] * 4
        + [pltpu.SMEM((heads,), jnp.int32)]
        + [pltpu.VMEM(rows, LOW)] * 4
        + [pltpu.VMEM(gain_dims, LOW)]
        + [pltpu.VMEM(master_gain.shape, F32)] * 3
        + [
            pltpu.VMEM(tile, F32),
            pltpu.VMEM((heads, length, length), F32),
            pltpu.VMEM((heads, length, length), LOW),
            pltpu.VMEM(state, LOW),
        ]
        + [pltpu.VMEM(state, F32)] * 5
        + [
            pltpu.VMEM(tile, LOW),
            pltpu.VMEM(gain_dims, F32),
            pltpu.VMEM(gain_dims, F32),
            pltpu.VMEM((length, HEAD_DIM), F32),
            pltpu.VMEM((length, HEAD_DIM), F32),
            pltpu.VMEM((8, length), F32),
            pltpu.VMEM((n_tensor - 1, 8, length), F32),
            pltpu.VMEM((n_ctx - 1,) + gain_dims, F32),
            pltpu.VMEM(gain_dims, F32),
            pltpu.VMEM((n_dp - 1,) + gain_dims, F32),
            dma((9,)),
            dma((1,)),
            dma((3, heads)),
        ]
        + [dma((heads, PARTS))] * 4
        + [dma((count - 1,)) for count in (n_tensor, n_tensor, n_ctx, n_ctx, n_dp, n_dp)]
    )
    out_shape = [jax.ShapeDtypeStruct(rows, LOW)] * 4 + [
        jax.ShapeDtypeStruct(master_gain.shape, F32)
    ] * 3
    held = pl.pallas_call(
        functools.partial(fused, (heads, length, n_dp, n_ctx, n_tensor)),
        out_shape=out_shape,
        in_specs=[hbm_spec] * 9,
        out_specs=[hbm_spec] * 4 + [vmem_spec] * 3,
        scratch_shapes=scratch,
        compiler_params=pltpu.CompilerParams(
            collective_id=0, has_side_effects=True, vmem_limit_bytes=67043328
        ),
        name="fused",
    )(
        decay_exp,
        query_rows.reshape(rows),
        key_rows.reshape(rows),
        value_rows.reshape(rows),
        out_grad.reshape(rows),
        gain_weight,
        master_gain,
        first_moment,
        second_moment,
    )
    results = pl.pallas_call(
        store_all,
        out_shape=out_shape,
        in_specs=[hbm_spec] * 7,
        out_specs=[hbm_spec] * 7,
        scratch_shapes=[pltpu.VMEM(part.shape, part.dtype) for part in out_shape] + [dma((2, 7))],
        compiler_params=pltpu.CompilerParams(vmem_limit_bytes=67043328),
        name="store_all",
    )(*held)
    full = tuple(part.reshape(query_rows.shape) for part in results[:4])
    return full + tuple(results[4:])


def solution(mesh):
    rows = P("dp", "ctx", "tensor")
    share = P("tensor", ("dp", "ctx"))
    mesh_dims = (mesh.shape["dp"], mesh.shape["ctx"], mesh.shape["tensor"])
    return jax.shard_map(
        functools.partial(body, mesh_dims),
        mesh=mesh,
        in_specs=(rows, rows, rows, P("tensor"), rows, P("tensor", None), share, share, share),
        out_specs=(rows, rows, rows, rows, share, share, share),
        check_vma=False,
    )
```

```python
import functools
import math

import jax
import jax.numpy as jnp
from jax import lax
from jax.experimental import pallas as pl
from jax.experimental.pallas import tpu as pltpu
from jax.sharding import PartitionSpec as P

HEAD_DIM = 128
PARTS = 2
MESH = pl.DeviceIdType.MESH

beta_one = 0.9
beta_two = 0.95
learn_rate = 0.02
adam_eps = 1e-08
bias_one = 0.9999734386011124
bias_two = 0.9940794707796667
norm_eps = 1e-05

LOW = jnp.bfloat16
F32 = jnp.float32


def dot(a, b, dim_a, dim_b, precision=None):
    return lax.dot_general(
        a, b, (((dim_a,), (dim_b,)), ((), ())), preferred_element_type=F32, precision=precision
    )


def fused(
    dims,
    exp_hbm,
    query_hbm,
    key_hbm,
    value_hbm,
    grad_hbm,
    gain_hbm,
    master_hbm,
    first_hbm,
    second_hbm,
    attn_out,
    qgrad_out,
    kgrad_out,
    vgrad_out,
    master_out,
    moment_out,
    second_out,
    exp_ref,
    query_v,
    key_v,
    value_v,
    grad_v,
    gain_ref,
    master_ref,
    first_ref,
    second_ref,
    attn_v,
    mask_v,
    weight_v,
    low_v,
    local_v,
    fwd_in,
    fwd_out,
    bwd_in,
    bwd_out,
    gl_v,
    gain_v,
    gpart_v,
    square_acc,
    dot_acc,
    norm_mine,
    norm_in,
    ctx_in,
    dp_mine,
    dp_in,
    in_sem,
    fs_sem,
    fr_sem,
    bs_sem,
    br_sem,
    ts_sem,
    tr_sem,
    cs_sem,
    cr_sem,
    ds_sem,
    dr_sem,
):
    heads, length, n_dp, n_ctx, n_tensor = dims
    seq_len = length * n_ctx
    channels = heads * HEAD_DIM * n_tensor
    token_count = n_dp * seq_len
    at_dp, at_ctx, at_tensor = (lax.axis_index(name) for name in ("dp", "ctx", "tensor"))
    later = lax.rem(at_ctx + 1, n_ctx)
    earlier = lax.rem(at_ctx + n_ctx - 1, n_ctx)
    is_first, is_last = at_ctx == 0, at_ctx == n_ctx - 1

    def columns(h):
        return pl.ds(pl.multiple_of(h * HEAD_DIM, HEAD_DIM), HEAD_DIM)

    pairs = (
        (exp_hbm, exp_ref),
        (key_hbm, key_v),
        (value_hbm, value_v),
        (query_hbm, query_v),
        (grad_hbm, grad_v),
        (gain_hbm, gain_ref),
        (master_hbm, master_ref),
        (first_hbm, first_ref),
        (second_hbm, second_ref),
    )
    loads = [
        pltpu.make_async_copy(hbm, local, in_sem.at[i]) for i, (hbm, local) in enumerate(pairs)
    ]
    def loop(low, high, step):
        lax.fori_loop(low, high, lambda h, c: (step(h), c)[1], 0)

    barrier = pltpu.get_barrier_semaphore()
    groups = (("dp", at_dp, n_dp), ("ctx", at_ctx, n_ctx), ("tensor", at_tensor, n_tensor))
    for name, mine, count in groups:
        for d in range(1, count):
            pl.semaphore_signal(
                barrier, inc=1, device_id={name: lax.rem(mine + d, count)}, device_id_type=MESH
            )
    for copy in loads:
        copy.start()

    def share(name, mine, count, source, slots, send_sem, recv_sem):
        return [
            pltpu.make_async_remote_copy(
                src_ref=source,
                dst_ref=slots.at[d - 1],
                send_sem=send_sem.at[d - 1],
                recv_sem=recv_sem.at[d - 1],
                device_id={name: lax.rem(mine + d, count)},
                device_id_type=MESH,
            )
            for d in range(1, count)
        ]

    part_rows = HEAD_DIM // PARTS

    def some_rows(part):
        return pl.ds(part * part_rows, part_rows)

    def forward_copy(h, part):
        return pltpu.make_async_remote_copy(
            src_ref=fwd_out.at[h, some_rows(part)],
            dst_ref=fwd_in.at[h, some_rows(part)],
            send_sem=fs_sem.at[h, part],
            recv_sem=fr_sem.at[h, part],
            device_id={"ctx": later},
            device_id_type=MESH,
        )

    def backward_copy(h, part):
        return pltpu.make_async_remote_copy(
            src_ref=bwd_out.at[h, some_rows(part)],
            dst_ref=bwd_in.at[h, some_rows(part)],
            send_sem=bs_sem.at[h, part],
            recv_sem=br_sem.at[h, part],
            device_id={"ctx": earlier},
            device_id_type=MESH,
        )

    row = lax.broadcasted_iota(jnp.int32, (length, HEAD_DIM), 0).astype(F32)

    def rate_of(h):
        return exp_ref[h].astype(F32) * (math.log(2.0) / (4.0 * seq_len))

    def key_decay(h):
        return jnp.exp(-rate_of(h) * (length - row))

    def query_decay(h):
        return jnp.exp(-rate_of(h) * row)

    def block_decay(h):
        return jnp.exp(jnp.full((part_rows, HEAD_DIM), -rate_of(h) * length, F32))

    def summarize(h):
        scaled = (key_decay(h) * key_v[:, columns(h)].astype(F32)).astype(LOW)
        summary = dot(scaled, value_v[:, columns(h)], 0, 0)

        @pl.when(is_first)
        def _():
            fwd_out[h] = summary

        @pl.when(jnp.logical_not(is_first))
        def _():
            local_v[h] = summary

    for copy in loads[:3]:
        copy.wait()
    loop(0, heads, summarize)
    pl.semaphore_wait(barrier, n_dp + n_ctx + n_tensor - 3)

    @pl.when(is_first)
    def _():
        def send(h):
            for part in range(PARTS):
                forward_copy(h, part).start()

        loop(0, heads, send)

    for copy in loads[3:]:
        copy.wait()
    gain_v[...] = gain_ref[...].astype(F32)
    square_acc[...] = jnp.zeros_like(square_acc)
    dot_acc[...] = jnp.zeros_like(dot_acc)

    def attend(h):
        gap = (
            lax.broadcasted_iota(jnp.int32, (length, length), 0)
            - lax.broadcasted_iota(jnp.int32, (length, length), 1)
        ).astype(F32)
        mask = jnp.where(gap >= 0, jnp.exp(-rate_of(h) * jnp.maximum(gap, 0.0)), 0.0)
        mask_v[h] = mask
        query = query_v[:, columns(h)]
        weights = (dot(query, key_v[:, columns(h)], 1, 1) * mask).astype(LOW)
        weight_v[h] = weights
        attn_v[h] = dot(weights, value_v[:, columns(h)], 1, 0)

        @pl.when(is_first)
        def _():
            low_v[h] = jnp.zeros((HEAD_DIM, HEAD_DIM), LOW)

        @pl.when(jnp.logical_not(is_first))
        def _():
            for part in range(PARTS):
                rows = some_rows(part)
                forward_copy(h, part).wait_recv()

                @pl.when(jnp.logical_not(is_last))
                def _():
                    fwd_out[h, rows] = block_decay(h) * fwd_in[h, rows] + local_v[h, rows]
                    forward_copy(h, part).start()

            low_v[h] = fwd_in[h].astype(LOW)

        attn = attn_v[h] + query_decay(h) * dot(query_v[:, columns(h)], low_v[h], 1, 0)
        attn_v[h] = attn
        square_acc[...] += attn * attn
        dot_acc[...] += grad_v[:, columns(h)].astype(F32) * gain_v[pl.ds(h, 1), :] * attn

    loop(0, heads, attend)

    exact = lax.Precision.HIGHEST
    ones = jnp.ones((8, HEAD_DIM), F32)
    upper = lax.broadcasted_iota(jnp.int32, (8, length), 0) < 4
    norm_mine[...] = jnp.where(
        upper, dot(ones, square_acc[...], 1, 1, exact), dot(ones, dot_acc[...], 1, 1, exact)
    )
    norm_copies = share("tensor", at_tensor, n_tensor, norm_mine, norm_in, ts_sem, tr_sem)
    for copy in norm_copies:
        copy.start()
    total = norm_mine[...]
    for d, copy in enumerate(norm_copies):
        copy.wait_recv()
        total = total + norm_in[d]
    pick = lax.broadcasted_iota(jnp.int32, (8, HEAD_DIM), 0)
    square_sum = dot(total, (pick == 0).astype(F32), 0, 0, exact)
    dot_sum = dot(total, (pick == 4).astype(F32), 0, 0, exact)
    inv_rms = lax.rsqrt(square_sum / channels + norm_eps)
    mean_dot = dot_sum / channels
    square_acc[...] = inv_rms
    dot_acc[...] = inv_rms * inv_rms * mean_dot

    early = min(3, heads)

    def back_summary(h):
        attn = attn_v[h]
        inverse = square_acc[...]
        gain = gain_v[pl.ds(h, 1), :]
        grad = grad_v[:, columns(h)].astype(F32)
        grad_low = (inverse * (grad * gain - attn * dot_acc[...])).astype(LOW)
        gl_v[h] = grad_low
        scaled = (query_decay(h) * query_v[:, columns(h)].astype(F32)).astype(LOW)
        part = dot(scaled, grad_low, 0, 0)

        @pl.when(is_last)
        def _():
            bwd_out[h] = part

            @pl.when(h < early)
            def _():
                for piece in range(PARTS):
                    backward_copy(h, piece).start()

        @pl.when(jnp.logical_not(is_last))
        def _():
            local_v[h] = part

        normed = attn * inverse
        attn_out[:, columns(h)] = (gain * normed).astype(LOW)
        gpart_v[pl.ds(h, 1), :] = jnp.sum(grad * normed, axis=0, keepdims=True)

    loop(0, heads, back_summary)
    ctx_copies = share("ctx", at_ctx, n_ctx, gpart_v, ctx_in, cs_sem, cr_sem)
    for copy in ctx_copies:
        copy.start()

    @pl.when(is_last)
    def _():
        def send(h):
            for part in range(PARTS):
                backward_copy(h, part).start()

        loop(early, heads, send)


    def gradients(h):
        grad_low = gl_v[h]
        dweights = (dot(grad_low, value_v[:, columns(h)], 1, 1) * mask_v[h]).astype(LOW)
        query_part = dot(dweights, key_v[:, columns(h)], 1, 0)
        query_part += query_decay(h) * dot(grad_low, low_v[h], 1, 1)
        qgrad_out[:, columns(h)] = query_part.astype(LOW)
        key_part = dot(dweights, query_v[:, columns(h)], 0, 0)
        value_part = dot(weight_v[h], grad_low, 0, 0)

        @pl.when(is_last)
        def _():
            kgrad_out[:, columns(h)] = key_part.astype(LOW)
            vgrad_out[:, columns(h)] = value_part.astype(LOW)

        @pl.when(jnp.logical_not(is_last))
        def _():
            for part in range(PARTS):
                rows = some_rows(part)
                backward_copy(h, part).wait_recv()

                @pl.when(jnp.logical_not(is_first))
                def _():
                    bwd_out[h, rows] = block_decay(h) * bwd_in[h, rows] + local_v[h, rows]
                    backward_copy(h, part).start()

            back_low = bwd_in[h].astype(LOW)
            decay = key_decay(h)
            kgrad_out[:, columns(h)] = (key_part + decay * dot(value_v[:, columns(h)], back_low, 1, 1)).astype(LOW)
            vgrad_out[:, columns(h)] = (value_part + decay * dot(key_v[:, columns(h)], back_low, 1, 0)).astype(LOW)


    loop(0, heads - 2, gradients)
    gain_sum = gpart_v[...]
    for d, copy in enumerate(ctx_copies):
        copy.wait_recv()
        gain_sum = gain_sum + ctx_in[d]
    dp_mine[...] = gain_sum
    dp_copies = share("dp", at_dp, n_dp, dp_mine, dp_in, ds_sem, dr_sem)
    for copy in dp_copies:
        copy.start()
    loop(heads - 2, heads, gradients)

    gain_sum = dp_mine[...]
    for d, copy in enumerate(dp_copies):
        copy.wait_recv()
        gain_sum = gain_sum + dp_in[d]
    width = master_ref.shape[1]
    place = (at_dp * n_ctx + at_ctx) * width
    chosen = lax.broadcasted_iota(jnp.int32, (HEAD_DIM, width), 0) == (
        lax.broadcasted_iota(jnp.int32, (HEAD_DIM, width), 1) + place
    )
    gain_grad = dot(gain_sum, chosen.astype(F32), 1, 0, exact) / math.sqrt(token_count)
    moment_new = beta_one * first_ref[...] + (1.0 - beta_one) * gain_grad
    second_new = beta_two * second_ref[...] + (1.0 - beta_two) * gain_grad * gain_grad
    moment_out[...] = moment_new
    second_out[...] = second_new
    master_out[...] = master_ref[...] - learn_rate * (moment_new / bias_one) / (
        jnp.sqrt(second_new / bias_two) + adam_eps
    )

    def finish(h):
        @pl.when(jnp.logical_not(is_last))
        def _():
            for part in range(PARTS):
                forward_copy(h, part).wait_send()

        @pl.when(jnp.logical_not(is_first))
        def _():
            for part in range(PARTS):
                backward_copy(h, part).wait_send()

    loop(0, heads, finish)
    for copy in norm_copies + ctx_copies + dp_copies:
        copy.wait_send()


def store_all(*refs):
    count = len(refs) // 2
    sems = refs[2 * count]
    copies = [
        pltpu.make_async_copy(source, target, sems.at[i])
        for i, (source, target) in enumerate(zip(refs[:count], refs[count : 2 * count]))
    ]
    for copy in copies:
        copy.start()
    for copy in copies:
        copy.wait()


def body(
    mesh_dims,
    query_rows,
    key_rows,
    value_rows,
    decay_exp,
    out_grad,
    gain_weight,
    master_gain,
    first_moment,
    second_moment,
):
    _, length, row_width = query_rows.shape
    heads = row_width // HEAD_DIM
    n_dp, n_ctx, n_tensor = mesh_dims
    rows = (length, row_width)
    tile = (heads, length, HEAD_DIM)
    state = (heads, HEAD_DIM, HEAD_DIM)
    gain_dims = (heads, HEAD_DIM)
    hbm_spec = pl.BlockSpec(memory_space=pltpu.HBM)
    vmem_spec = pl.BlockSpec(memory_space=pltpu.VMEM)
    dma = pltpu.SemaphoreType.DMA
    scratch = (
        [pltpu.SMEM((heads,), jnp.int32)]
        + [pltpu.VMEM(rows, LOW)] * 4
        + [pltpu.VMEM(gain_dims, LOW)]
        + [pltpu.VMEM(master_gain.shape, F32)] * 3
        + [
            pltpu.VMEM(tile, F32),
            pltpu.VMEM((heads, length, length), F32),
            pltpu.VMEM((heads, length, length), LOW),
            pltpu.VMEM(state, LOW),
        ]
        + [pltpu.VMEM(state, F32)] * 5
        + [
            pltpu.VMEM(tile, LOW),
            pltpu.VMEM(gain_dims, F32),
            pltpu.VMEM(gain_dims, F32),
            pltpu.VMEM((length, HEAD_DIM), F32),
            pltpu.VMEM((length, HEAD_DIM), F32),
            pltpu.VMEM((8, length), F32),
            pltpu.VMEM((n_tensor - 1, 8, length), F32),
            pltpu.VMEM((n_ctx - 1,) + gain_dims, F32),
            pltpu.VMEM(gain_dims, F32),
            pltpu.VMEM((n_dp - 1,) + gain_dims, F32),
            dma((9,)),
        ]
        + [dma((heads, PARTS))] * 4
        + [dma((count - 1,)) for count in (n_tensor, n_tensor, n_ctx, n_ctx, n_dp, n_dp)]
    )
    out_shape = [jax.ShapeDtypeStruct(rows, LOW)] * 4 + [
        jax.ShapeDtypeStruct(master_gain.shape, F32)
    ] * 3
    held = pl.pallas_call(
        functools.partial(fused, (heads, length, n_dp, n_ctx, n_tensor)),
        out_shape=[pltpu.VMEM(part.shape, part.dtype) for part in out_shape],
        in_specs=[hbm_spec] * 9,
        out_specs=[vmem_spec] * 7,
        scratch_shapes=scratch,
        compiler_params=pltpu.CompilerParams(
            collective_id=0, has_side_effects=True, vmem_limit_bytes=61*1024*1024
        ),
        name="fused",
    )(
        decay_exp,
        query_rows.reshape(rows),
        key_rows.reshape(rows),
        value_rows.reshape(rows),
        out_grad.reshape(rows),
        gain_weight,
        master_gain,
        first_moment,
        second_moment,
    )
    results = pl.pallas_call(
        store_all,
        out_shape=out_shape,
        in_specs=[vmem_spec] * 7,
        out_specs=[hbm_spec] * 7,
        scratch_shapes=[dma((7,))],
        compiler_params=pltpu.CompilerParams(vmem_limit_bytes=1024 * 1024),
        name="store_all",
    )(*held)
    full = tuple(part.reshape(query_rows.shape) for part in results[:4])
    return full + tuple(results[4:])


def solution(mesh):
    rows = P("dp", "ctx", "tensor")
    share = P("tensor", ("dp", "ctx"))
    mesh_dims = (mesh.shape["dp"], mesh.shape["ctx"], mesh.shape["tensor"])
    return jax.shard_map(
        functools.partial(body, mesh_dims),
        mesh=mesh,
        in_specs=(rows, rows, rows, P("tensor"), rows, P("tensor", None), share, share, share),
        out_specs=(rows, rows, rows, rows, share, share, share),
        check_vma=False,
    )
```
